32 devices in a mesh: section: 2 (over core), ctx: 16 (over z, y, x).
Axes of the slice: x: 2, y: 2, z: 4, core: 2. Of those that a mesh axis runs over, the one named last changes fastest.
Arguments:
- tokens: bfloat16 [2, 2048, 2048], P(None, 'ctx'), may hold values from -6 to 6
- qkv_weight: bfloat16 [2, 2048, 3072], P('section', 'ctx'), may hold values from -0.125 to 0.125
- out_weight: bfloat16 [2, 1024, 2048], P('section', 'ctx'), may hold values from -0.1875 to 0.1875
- log_decay: float32 [2, 2, 2048, 16], P('section', None, 'ctx'), may hold values from -1.5 to 0, as said below
Outputs:
- hidden_states: bfloat16 [2, 2, 2048, 2048], P('section', None, 'ctx')
The draws below stay inside these ranges and needn't reach their ends.
Inputs may be any that keep to these rules, and one draw needn't show every extreme that they name: `log_decay`: every value is negative.
All inputs are finite; a program needn't handle non-finite values.
Results may differ from the reference program's by a relative error of at most 0.025.
Values may be sent and summed in bfloat16 or wider, within the bound.
A program may use at most 128 MiB of HBM per device.

```python
import jax
import jax.numpy as jnp
from jax import lax

D = 2048
MIXER_HEADS = 16
HEAD = 64
TOK_DEV = 128
MICRO_BATCHES = 2
LAYER_TOTAL = 2
SEQUENCE_LENGTH = 2048
N_CTX = 16


def draw_log_decay(key, part):
    key_rows_list = jax.random.split(key, 7)
    slow_share = 0.5
    head_shape = (LAYER_TOTAL, 1, 1, 1, MIXER_HEADS)
    slow_heads = jax.random.bernoulli(key_rows_list[0], slow_share, head_shape)
    fast_rate = jax.random.uniform(key_rows_list[1], head_shape, jnp.float32, 1.0 / 50.0, 1.0 / 30.0)
    slow_total = jax.random.uniform(key_rows_list[2], head_shape, jnp.float32, 0.1, 0.45)
    base_rate = jnp.where(slow_heads, slow_total / SEQUENCE_LENGTH, fast_rate)
    device_factor = jax.random.uniform(key_rows_list[3], (LAYER_TOTAL, MICRO_BATCHES, N_CTX, 1, MIXER_HEADS), jnp.float32, 0.6, 1.4)
    position_factor = jnp.clip(1.0 + 0.2 * jax.random.normal(key_rows_list[4], (LAYER_TOTAL, MICRO_BATCHES, N_CTX, TOK_DEV, MIXER_HEADS), jnp.float32), 0.6, 1.4)
    decay_rate = (base_rate * device_factor * position_factor).reshape(LAYER_TOTAL, MICRO_BATCHES, SEQUENCE_LENGTH, MIXER_HEADS)
    spurt_position_list = jax.random.randint(key_rows_list[5], (LAYER_TOTAL, MICRO_BATCHES, 2), 0, SEQUENCE_LENGTH)
    spurt_keep_mask = jax.random.uniform(key_rows_list[6], (LAYER_TOTAL, MICRO_BATCHES, 2, MIXER_HEADS), jnp.float32, 0.5, 0.8)
    position_index = jnp.arange(SEQUENCE_LENGTH, dtype=jnp.int32)
    match_count = (position_index[None, None, None, :] == spurt_position_list[:, :, :, None]).astype(jnp.float32)
    spurt_state_sum = jnp.einsum('kgay,kgae->kgye', match_count, jnp.log(spurt_keep_mask))
    return -decay_rate + spurt_state_sum


def block_levels(own_key, shape, cuts, least, largest):
    def one(dim, blocks):
        heights = jax.random.uniform(jax.random.fold_in(jax.random.fold_in(own_key, 6), dim), (blocks,), jnp.float32, least / len(cuts), largest / len(cuts))
        return jnp.repeat(jnp.exp(heights), shape[dim] // blocks).reshape((-1,) + (1,) * (len(shape) - dim - 1))

    gain = one(*cuts[0])
    for cut in cuts[1:]:
        gain = gain * one(*cut)
    return gain


def noise(rng, shape, spread, reach, pieces=(), kind=jnp.bfloat16):
    gain = block_levels(rng, shape, pieces, -0.22, 0.18) if pieces else 1.0
    entries = jax.random.normal(rng, shape, jnp.float32) * spread * gain
    return jnp.minimum(jnp.maximum(entries, -reach), reach).astype(kind)


def setup_inputs(seed: int = 0) -> dict:
    key_of = jax.random.split(jax.random.key(seed), 5)
    tokens = noise(key_of[0], (MICRO_BATCHES, SEQUENCE_LENGTH, D), 1.0, 6.0, ((1, 16),))
    qkv_weight = noise(key_of[1], (LAYER_TOTAL, D, 3 * MIXER_HEADS * HEAD), D ** -0.5, 0.125, ((0, 2), (1, 16)))
    out_weight = noise(key_of[2], (LAYER_TOTAL, MIXER_HEADS * HEAD, D), (MIXER_HEADS * HEAD) ** -0.5, 0.1875, ((0, 2), (1, 16)))
    log_decay = draw_log_decay(jax.random.fold_in(key_of[4], 71), 0)
    return {"tokens": tokens, "qkv_weight": qkv_weight, "out_weight": out_weight, "log_decay": log_decay}


def round_low(value_rows):
    return lax.optimization_barrier(value_rows.astype(jnp.bfloat16)).astype(jnp.float32)

def apply_layer(inputs, weight, out_proj, decay):
    seq_len, model_width = inputs.shape
    head_count = decay.shape[1]
    wide_input = inputs.astype(jnp.float32)
    normed = (wide_input * lax.rsqrt(lax.optimization_barrier(jnp.mean(wide_input * wide_input, axis=-1, keepdims=True)) + 1e-05)).astype(jnp.bfloat16)
    projected = jnp.dot(normed, weight, preferred_element_type=jnp.float32).astype(jnp.bfloat16)
    inner = projected.shape[1] // 3
    head_dim = inner // head_count
    blocks = seq_len // TOK_DEV
    query_rows = projected[:, :inner].reshape(blocks, TOK_DEV, head_count, head_dim).astype(jnp.float32)
    key_block = projected[:, inner:2 * inner].reshape(blocks, TOK_DEV, head_count, head_dim).astype(jnp.float32)
    value_rows = projected[:, 2 * inner:].reshape(blocks, TOK_DEV, head_count, head_dim).astype(jnp.float32)
    cumulative = jnp.cumsum(decay.reshape(blocks, TOK_DEV, head_count), axis=1)
    ending = cumulative[:, -1]
    key_rows_scaled = round_low(key_block * jnp.exp(ending[:, None, :] - cumulative)[..., None])
    block_state = jnp.einsum('bjhk,bjhv->bhkv', key_rows_scaled, value_rows)
    totals = jnp.exp(ending)

    def carry_step(carried, block_item):
        block_total, state_here = block_item
        return (block_total[:, None, None] * carried + state_here, carried)
    start = jnp.zeros((head_count, head_dim, head_dim), jnp.float32)
    _, carried = lax.scan(carry_step, start, (totals, block_state))
    carried_state_low = round_low(carried)
    scores = jnp.einsum('bthk,bjhk->bhtj', query_rows, key_block)
    per_head = jnp.transpose(cumulative, (0, 2, 1))
    decay_gap = per_head[:, :, :, None] - per_head[:, :, None, :]
    position_index = jnp.arange(TOK_DEV, dtype=jnp.int32)
    causal = position_index[:, None] >= position_index[None, :]
    weights = round_low(jnp.where(causal, scores * jnp.exp(jnp.where(causal, decay_gap, 0.0)), 0.0))
    intra_out = jnp.einsum('bhtj,bjhv->bthv', weights, value_rows)
    inter_out = jnp.einsum('bthk,bhkv->bthv', query_rows, carried_state_low) * jnp.exp(cumulative)[..., None]
    mixture = intra_out + inter_out
    normed_out = mixture * lax.rsqrt(lax.optimization_barrier(jnp.mean(mixture * mixture, axis=-1, keepdims=True)) + 1e-05)
    mixed_low = normed_out.reshape(seq_len, inner).astype(jnp.bfloat16)
    mixed = jnp.dot(mixed_low, out_proj, preferred_element_type=jnp.float32)
    return (wide_input + mixed).astype(jnp.bfloat16)

def reference(tokens, qkv_weight, out_weight, log_decay):
    layer_outputs = []
    current = [tokens[micro_index] for micro_index in range(MICRO_BATCHES)]
    for layer_index in range(LAYER_TOTAL):
        current = [apply_layer(current[micro_index], qkv_weight[layer_index], out_weight[layer_index], log_decay[layer_index, micro_index]) for micro_index in range(MICRO_BATCHES)]
        layer_outputs.append(jnp.stack(current, axis=0))
    return jnp.stack(layer_outputs, axis=0)
```

```python
import functools

import jax
import jax.numpy as jnp
import numpy as np
from jax import lax
from jax.experimental import pallas as pl
from jax.experimental.pallas import tpu as pltpu
from jax.sharding import PartitionSpec as P

MESH = pl.DeviceIdType.MESH
TILE = 16


def line_sizes(mesh):
    total = mesh.shape["ctx"]
    places = np.moveaxis(mesh.devices, mesh.axis_names.index("ctx"), 0).reshape(total, -1)[:, 0]
    sizes, left = [], total
    try:
        coords = [tuple(d.coords) for d in places]
    except AttributeError:
        coords = None
    if coords is not None:
        step = 1
        while step < total:
            changed = [a != b for a, b in zip(coords[0], coords[step])]
            axis = changed.index(True)
            size = 1
            while step * size < total and (
                size == 1 or (coords[step * size][axis] != coords[0][axis]
                and all(coords[step * size][i] == coords[0][i] for i in range(3) if i != axis))
            ):
                size += 1
            while total % (step * size):
                size -= 1
            sizes.insert(0, size)
            step *= size
    else:
        while left > 1:
            sizes.append(2)
            left //= 2
    return tuple(sizes)


def routes(sizes):
    d = len(sizes)
    if d != 3:
        return [(tuple(range(d)), 1)]
    return [((0, 2, 1), 3), ((0, 1, 2), 3), ((2, 1, 0), 1), ((1, 2, 0), 1)]


def pieces(rows, sizes):
    orders = routes(sizes)
    units = rows // TILE
    if len(orders) == 1 or units < 2:
        return [(orders[0][0], 0, rows)]
    shares = [units // 2, units - units // 2] if units < 8 else None
    if shares is None:
        whole = sum(s for _, s in orders)
        shares = [s * units // whole for _, s in orders]
        shares[0] += units - sum(shares)
    out, at = [], 0
    for (order, _), share in zip(orders, shares):
        out.append((order, at * TILE, share * TILE))
        at += share
    return out


def place_in_line(me, size, t):
    low = jnp.minimum(me, size - 1 - me)
    half = lax.div(t + 1, 2)
    near = jnp.where(lax.rem(t, 2) == 1, me + half, me - half)
    far = jnp.where(me < size - 1 - me, me + (t - low), me - (t - low))
    return jnp.where(t <= 2 * low, near, far)


def gather_kernel(sizes, plan, *refs):
    count = len(plan)
    shards, wholes = refs[:count], refs[count : 2 * count]
    send_sem, recv_sem, own_sem = refs[2 * count :]
    d = len(sizes)
    total = int(np.prod(sizes))
    strides = [int(np.prod(sizes[i + 1 :])) for i in range(d)]
    me = lax.axis_index("ctx")
    mine = [lax.rem(lax.div(me, strides[i]), sizes[i]) for i in range(d)]
    slots, ways = 0, []
    for i in range(d):
        for sign in (1, -1):
            ways.append((i, sign, slots if sizes[i] == 2 or sign == 1 else slots + 1))
        slots += 1 if sizes[i] == 2 else 2

    barrier = pltpu.get_barrier_semaphore()
    near = jnp.int32(0)
    for i, sign, _ in ways:
        there = jnp.logical_and(mine[i] + sign >= 0, mine[i] + sign < sizes[i])
        near = near + there.astype(jnp.int32)

        @pl.when(there)
        def _(i=i, sign=sign):
            pl.semaphore_signal(
                barrier, inc=1, device_id={"ctx": me + sign * strides[i]}, device_id_type=MESH
            )

    pl.semaphore_wait(barrier, near)

    parts = [(a, order, at, rows) for a in range(count) for order, at, rows in plan[a]]

    def copy(source, index, way, own):
        a, _, at, rows = parts[index]
        i, sign, slot = way
        depth = shards[a].shape[0]
        begin = pl.multiple_of(source * depth + at, TILE)
        target = wholes[a].at[pl.ds(begin, rows)]
        return pltpu.make_async_remote_copy(
            src_ref=shards[a].at[pl.ds(at, rows)] if own else target,
            dst_ref=target,
            send_sem=send_sem.at[source, index, slot],
            recv_sem=recv_sem.at[source, index],
            device_id={"ctx": me + sign * strides[i]},
            device_id_type=MESH,
        )

    def onward(source, coords, index, own, act):
        order = parts[index][1]
        for way in ways:
            i, sign, _ = way
            ok = jnp.logical_and(mine[i] + sign >= 0, mine[i] + sign < sizes[i])
            if not own:
                here = coords[i]
                ok = jnp.logical_and(ok, (mine[i] - here) * sign >= 0)
                for later in order[order.index(i) + 1 :]:
                    ok = jnp.logical_and(ok, mine[later] == coords[later])

            @pl.when(ok)
            def _(way=way):
                act(copy(source, index, way, own))

    for index in range(len(parts)):
        onward(me, mine, index, True, lambda c: c.start())
    own_copies = []
    for a in range(count):
        depth = shards[a].shape[0]
        own_copies.append(
            pltpu.make_async_copy(
                shards[a],
                wholes[a].at[pl.ds(pl.multiple_of(me * depth, TILE), depth)],
                own_sem.at[a],
            )
        )
        own_copies[-1].start()

    def source_of(j):
        coords = [
            place_in_line(mine[i], sizes[i], lax.rem(lax.div(j, strides[i]), sizes[i]))
            for i in range(d)
        ]
        source = sum(c * s for c, s in zip(coords, strides))
        return source, coords

    @pl.loop(1, total)
    def _(j):
        source, coords = source_of(j)
        for index in range(len(parts)):
            copy(source, index, ways[0], False).wait_recv()
            onward(source, coords, index, False, lambda c: c.start())

    for c in own_copies:
        c.wait()
    for index in range(len(parts)):
        onward(me, mine, index, True, lambda c: c.wait_send())

    @pl.loop(1, total)
    def _(j):
        source, coords = source_of(j)
        for index in range(len(parts)):
            onward(source, coords, index, False, lambda c: c.wait_send())


def gather_weights(sizes, *shards):
    total = int(np.prod(sizes))
    plan = [pieces(s.shape[0], sizes) for s in shards]
    parts = sum(len(p) for p in plan)
    slots = sum(1 if s == 2 else 2 for s in sizes)
    return pl.pallas_call(
        functools.partial(gather_kernel, sizes, plan),
        out_shape=[jax.ShapeDtypeStruct((s.shape[0] * total, s.shape[1]), s.dtype) for s in shards],
        in_specs=[pl.BlockSpec(memory_space=pl.ANY)] * len(shards),
        out_specs=[pl.BlockSpec(memory_space=pl.ANY)] * len(shards),
        scratch_shapes=[
            pltpu.SemaphoreType.DMA((total, parts, slots)),
            pltpu.SemaphoreType.DMA((total, parts)),
            pltpu.SemaphoreType.DMA((len(shards),)),
        ],
        compiler_params=pltpu.CompilerParams(collective_id=0, has_side_effects=True),
        name="gather_weights",
    )(*shards)


def carry_kernel(total, rows, send_ref, out_ref, got, carried, landed, s1, r1, s2, r2):
    me = lax.axis_index("ctx")
    barrier = pltpu.get_barrier_semaphore()

    @pl.loop(1, total)
    def _(k):
        pl.semaphore_signal(
            barrier, inc=1, device_id={"ctx": lax.rem(me + k, total)}, device_id_type=MESH
        )

    pl.semaphore_wait(barrier, total - 1)

    def first(to, slot_from):
        return pltpu.make_async_remote_copy(
            src_ref=send_ref.at[to],
            dst_ref=got.at[slot_from],
            send_sem=s1.at[to],
            recv_sem=r1.at[slot_from],
            device_id={"ctx": to},
            device_id_type=MESH,
        )

    def second(to, slot_from):
        return pltpu.make_async_remote_copy(
            src_ref=carried.at[to],
            dst_ref=landed.at[slot_from],
            send_sem=s2.at[to],
            recv_sem=r2.at[slot_from],
            device_id={"ctx": to},
            device_id_type=MESH,
        )

    @pl.loop(1, total)
    def _(k):
        first(lax.rem(me + k, total), me).start()

    got[me] = send_ref[me]

    def step(b, acc):
        @pl.when(b != me)
        def _():
            first(b, b).wait_recv()

        low = acc.astype(jnp.bfloat16)
        carried[b] = low

        @pl.when(b != me)
        def _():
            second(b, me).start()

        @pl.when(b == me)
        def _():
            landed[me] = low

        item = got[b].astype(jnp.float32)
        return acc * item[rows : rows + 1] + item[:rows]

    lax.fori_loop(0, total, step, jnp.zeros((rows, out_ref.shape[2]), jnp.float32))

    @pl.loop(1, total)
    def _(k):
        peer = lax.rem(me + k, total)
        first(peer, me).wait_send()
        second(peer, me).wait_send()
        second(peer, peer).wait_recv()

    out_ref[...] = landed[...]


def carry(total, items, call_id):
    rows = items.shape[1] - TILE
    lanes = items.shape[2]
    return pl.pallas_call(
        functools.partial(carry_kernel, total, rows),
        out_shape=jax.ShapeDtypeStruct((total, rows, lanes), jnp.bfloat16),
        in_specs=[pl.BlockSpec(memory_space=pltpu.VMEM)],
        out_specs=pl.BlockSpec(memory_space=pltpu.VMEM),
        scratch_shapes=[
            pltpu.VMEM((total, rows + TILE, lanes), jnp.bfloat16),
            pltpu.VMEM((total, rows, lanes), jnp.bfloat16),
            pltpu.VMEM((total, rows, lanes), jnp.bfloat16),
            pltpu.SemaphoreType.DMA((total,)),
            pltpu.SemaphoreType.DMA((total,)),
            pltpu.SemaphoreType.DMA((total,)),
            pltpu.SemaphoreType.DMA((total,)),
        ],
        compiler_params=pltpu.CompilerParams(collective_id=1, has_side_effects=True),
        name="carry_states",
    )(items)


def normalize_rows(value_rows):
    return value_rows * lax.rsqrt(jnp.mean(value_rows * value_rows, axis=-1, keepdims=True) + 1e-05)


def layer(total, incoming, weight_full, out_full, decay):
    micro, row_count, model_width = incoming.shape
    heads = decay.shape[2]
    wide = incoming.astype(jnp.float32)
    normed = normalize_rows(wide).astype(jnp.bfloat16).reshape(micro * row_count, model_width)
    projected = jnp.dot(normed, weight_full, preferred_element_type=jnp.float32).astype(
        jnp.bfloat16
    )
    inner = projected.shape[1] // 3
    head_dim = inner // heads
    q = projected[:, :inner].reshape(micro, row_count, heads, head_dim)
    k = projected[:, inner : 2 * inner].reshape(micro, row_count, heads, head_dim)
    v = projected[:, 2 * inner :].reshape(micro, row_count, heads, head_dim)
    cumul = jnp.cumsum(decay, axis=1)
    ending = cumul[:, -1]
    scaled = (k.astype(jnp.float32) * jnp.exp(ending[:, None, :] - cumul)[..., None]).astype(
        jnp.bfloat16
    )
    state = jnp.einsum("mthk,mthv->mhkv", scaled, v, preferred_element_type=jnp.float32)
    rows = heads * head_dim // total
    flat = state.astype(jnp.bfloat16).transpose(1, 2, 0, 3).reshape(total, rows, micro * head_dim)
    totals = jnp.exp(ending).astype(jnp.bfloat16)
    totals = jnp.broadcast_to(
        totals.T[:, None, :, None], (heads, head_dim, micro, head_dim)
    ).reshape(total, rows, micro * head_dim)[:, :1]
    items = jnp.concatenate(
        [flat, jnp.broadcast_to(totals, (total, TILE, micro * head_dim))], axis=1
    )
    low = carry(total, items, 1)
    carried = low.reshape(heads, head_dim, micro, head_dim)
    scores = jnp.einsum("mthk,mjhk->mhtj", q, k, preferred_element_type=jnp.float32)
    per_head = cumul.transpose(0, 2, 1)
    gap = per_head[..., :, None] - per_head[..., None, :]
    at = jnp.arange(row_count, dtype=jnp.int32)
    causal = at[:, None] >= at[None, :]
    weights = jnp.where(causal, scores * jnp.exp(jnp.where(causal, gap, 0.0)), 0.0).astype(
        jnp.bfloat16
    )
    intra = jnp.einsum("mhtj,mjhv->mthv", weights, v, preferred_element_type=jnp.float32)
    inter = (
        jnp.einsum("mthk,hkmv->mthv", q, carried, preferred_element_type=jnp.float32)
        * jnp.exp(cumul)[..., None]
    )
    mixed = normalize_rows(intra + inter).reshape(micro * row_count, inner).astype(jnp.bfloat16)
    product = jnp.dot(mixed, out_full, preferred_element_type=jnp.float32)
    return (wide + product.reshape(micro, row_count, model_width)).astype(jnp.bfloat16)


def shards(sizes, tokens, qkv_weight, out_weight, log_decay):
    sections = lax.axis_size("section")
    total = lax.axis_size("ctx")
    section_id = lax.axis_index("section")
    weight_full, out_full = gather_weights(sizes, qkv_weight[0], out_weight[0])
    result = tokens
    kept = tokens
    for stage in range(sections):
        result = layer(total, result, weight_full, out_full, log_decay[0])
        kept = jnp.where(section_id == stage, result, kept)
        if stage < sections - 1:
            result = lax.ppermute(
                result, "section", [(i, i + 1) for i in range(sections - 1)]
            )
    return kept[None]


def solution(mesh):
    in_specs = (
        P(None, "ctx", None),
        P("section", "ctx", None),
        P("section", "ctx", None),
        P("section", None, "ctx", None),
    )
    out_specs = P("section", None, "ctx", None)
    return jax.shard_map(
        functools.partial(shards, line_sizes(mesh)),
        mesh=mesh,
        in_specs=in_specs,
        out_specs=out_specs,
        check_vma=False,
    )
```

```python
import functools

import jax
import jax.numpy as jnp
import numpy as np
from jax import lax
from jax.experimental import pallas as pl
from jax.experimental.pallas import tpu as pltpu
from jax.sharding import PartitionSpec as P

MESH = pl.DeviceIdType.MESH
TILE = 16


def line_sizes(mesh):
    total = mesh.shape["ctx"]
    places = np.moveaxis(mesh.devices, mesh.axis_names.index("ctx"), 0).reshape(total, -1)[:, 0]
    sizes, left = [], total
    try:
        coords = [tuple(d.coords) for d in places]
    except AttributeError:
        coords = None
    if coords is not None:
        step = 1
        while step < total:
            changed = [a != b for a, b in zip(coords[0], coords[step])]
            axis = changed.index(True)
            size = 1
            while step * size < total and (
                size == 1 or (coords[step * size][axis] != coords[0][axis]
                and all(coords[step * size][i] == coords[0][i] for i in range(3) if i != axis))
            ):
                size += 1
            while total % (step * size):
                size -= 1
            sizes.insert(0, size)
            step *= size
    else:
        while left > 1:
            sizes.append(2)
            left //= 2
    return tuple(sizes)


def routes(sizes):
    d = len(sizes)
    if d != 3:
        return [(tuple(range(d)), 1)]
    return [((0, 2, 1), 3), ((0, 1, 2), 3), ((2, 1, 0), 1), ((1, 2, 0), 1)]


def pieces(rows, sizes):
    orders = routes(sizes)
    units = rows // TILE
    if len(orders) == 1 or units < 2:
        return [(orders[0][0], 0, rows)]
    shares = [units // 2, units - units // 2] if units < 8 else None
    if shares is None:
        whole = sum(s for _, s in orders)
        shares = [s * units // whole for _, s in orders]
        shares[0] += units - sum(shares)
    out, at = [], 0
    for (order, _), share in zip(orders, shares):
        out.append((order, at * TILE, share * TILE))
        at += share
    return out


def place_in_line(me, size, t):
    low = jnp.minimum(me, size - 1 - me)
    half = lax.div(t + 1, 2)
    near = jnp.where(lax.rem(t, 2) == 1, me + half, me - half)
    far = jnp.where(me < size - 1 - me, me + (t - low), me - (t - low))
    return jnp.where(t <= 2 * low, near, far)


def dot(a, b, contract=((1,), (0,)), precision=None):
    return lax.dot_general(
        a, b, (contract, ((), ())), precision=precision, preferred_element_type=jnp.float32
    )


def whole_kernel(
    sizes, sections, plan, heads, tokens, decay, shard_a, shard_b, out,
    full_a, full_b, xbuf, normed, proj, cumx, cumt, intra, mixed, result, items, got, carried,
    landed, send_sem, recv_sem, own_sem, x_send, x_recv, start_sem, s1, r1, s2, r2,
):
    f32, bf16 = jnp.float32, jnp.bfloat16
    shards, wholes = (shard_a, shard_b), (full_a, full_b)
    count = 2
    d = len(sizes)
    total = int(np.prod(sizes))
    strides = [int(np.prod(sizes[i + 1 :])) for i in range(d)]
    me = lax.axis_index("ctx")
    section = lax.axis_index("section")
    mine = [lax.rem(lax.div(me, strides[i]), sizes[i]) for i in range(d)]
    slots, ways = 0, []
    for i in range(d):
        for sign in (1, -1):
            ways.append((i, sign, slots if sizes[i] == 2 or sign == 1 else slots + 1))
        slots += 1 if sizes[i] == 2 else 2
    micro, rows, width = xbuf.shape
    inner = mixed.shape[1]
    head_dim = inner // heads
    pairs = heads // 2
    lanes = 2 * head_dim
    part = items.shape[1] - TILE

    barrier = pltpu.get_barrier_semaphore()

    @pl.loop(1, total)
    def _(k):
        pl.semaphore_signal(
            barrier, inc=1, device_id={"ctx": lax.rem(me + k, total)}, device_id_type=MESH
        )

    @pl.when(section > 0)
    def _():
        pl.semaphore_signal(barrier, inc=1, device_id={"section": section - 1}, device_id_type=MESH)

    @pl.when(section < sections - 1)
    def _():
        pl.semaphore_signal(barrier, inc=1, device_id={"section": section + 1}, device_id_type=MESH)

    greeted = (section > 0).astype(jnp.int32) + (section < sections - 1).astype(jnp.int32)
    pl.semaphore_wait(barrier, greeted + (total - 1))

    parts = [(a, order, at, size) for a in range(count) for order, at, size in plan[a]]

    def copy(source, index, way, own):
        a, _, at, size = parts[index]
        i, sign, slot = way
        depth = shards[a].shape[0]
        begin = pl.multiple_of(source * depth + at, TILE)
        target = wholes[a].at[pl.ds(begin, size)]
        return pltpu.make_async_remote_copy(
            src_ref=shards[a].at[pl.ds(at, size)] if own else target,
            dst_ref=target,
            send_sem=send_sem.at[source, index, slot],
            recv_sem=recv_sem.at[source, index],
            device_id={"ctx": me + sign * strides[i]},
            device_id_type=MESH,
        )

    def onward(source, coords, index, own, act):
        order = parts[index][1]
        for way in ways:
            i, sign, _ = way
            ok = jnp.logical_and(mine[i] + sign >= 0, mine[i] + sign < sizes[i])
            if not own:
                here = coords[i]
                ok = jnp.logical_and(ok, (mine[i] - here) * sign >= 0)
                for later in order[order.index(i) + 1 :]:
                    ok = jnp.logical_and(ok, mine[later] == coords[later])

            @pl.when(ok)
            def _(way=way):
                act(copy(source, index, way, own))

    own_copies = []
    for a in range(count):
        depth = shards[a].shape[0]
        own_copies.append(
            pltpu.make_async_copy(
                shards[a],
                wholes[a].at[pl.ds(pl.multiple_of(me * depth, TILE), depth)],
                own_sem.at[a],
            )
        )
        own_copies[-1].start()

    x_own = pltpu.make_async_copy(tokens, xbuf, own_sem.at[2])

    @pl.when(section == 0)
    def _():
        x_own.start()

    @pl.when(section > 0)
    def _():
        pl.semaphore_wait(start_sem, 1)

    for index in range(len(parts)):
        onward(me, mine, index, True, lambda c: c.start())

    at_row = lax.broadcasted_iota(jnp.int32, (rows, rows), 0)
    at_col = lax.broadcasted_iota(jnp.int32, (rows, rows), 1)
    causal = at_row >= at_col
    lower = causal.astype(f32)
    for m in range(micro):
        spread = (
            lax.broadcasted_iota(jnp.int32, (heads, heads * lanes), 0)
            == lax.broadcasted_iota(jnp.int32, (heads, heads * lanes), 1) // lanes
        ).astype(f32)
        own = decay[m]
        summed = dot(lower, own, precision=lax.Precision.HIGHEST)
        cumx[m] = dot(summed, spread, precision=lax.Precision.HIGHEST)
        cumt[m] = dot(own.T, lower, ((1,), (1,)), precision=lax.Precision.HIGHEST)

    def source_of(j):
        coords = [
            place_in_line(mine[i], sizes[i], lax.rem(lax.div(j, strides[i]), sizes[i]))
            for i in range(d)
        ]
        source = sum(c * s for c, s in zip(coords, strides))
        return source, coords

    @pl.loop(1, total)
    def _(j):
        source, coords = source_of(j)
        for index in range(len(parts)):
            copy(source, index, ways[0], False).wait_recv()
            onward(source, coords, index, False, lambda c: c.start())

        @pl.when(jnp.logical_and(j == total - GATE, section < sections - 1))
        def _():
            pl.semaphore_signal(
                start_sem, inc=1, device_id={"section": section + 1}, device_id_type=MESH
            )

    for c in own_copies:
        c.wait()

    pass_on = pltpu.make_async_remote_copy(
        src_ref=result,
        dst_ref=xbuf,
        send_sem=x_send.at[0],
        recv_sem=x_recv.at[0],
        device_id={"section": lax.rem(section + 1, sections)},
        device_id_type=MESH,
    )

    @pl.when(section == 0)
    def _():
        x_own.wait()

    @pl.when(section > 0)
    def _():
        pass_on.wait_recv()

    for m in range(micro):

        @pl.loop(0, rows // TILE)
        def _(r, m=m):
            at = pl.multiple_of(r * TILE, TILE)
            wide = xbuf[m, pl.ds(at, TILE), :].astype(f32)
            scale = lax.rsqrt(jnp.mean(wide * wide, axis=-1, keepdims=True) + 1e-05)
            normed[pl.ds(pl.multiple_of(m * rows + at, TILE), TILE), :] = (wide * scale).astype(bf16)

    @pl.loop(0, 3 * inner // 256)
    def _(c):
        cols = pl.ds(pl.multiple_of(c * 256, 256), 256)
        proj[:, cols] = dot(normed[...], full_a[:, cols]).astype(bf16)

    first_half = lax.broadcasted_iota(jnp.int32, (rows, lanes), 1) < head_dim
    first_item = lax.broadcasted_iota(jnp.int32, (head_dim, lanes), 1) < head_dim
    per_pair = head_dim // part

    def located(u):
        m, p = lax.div(u, pairs), lax.rem(u, pairs)
        span = pl.ds(pl.multiple_of(m * rows, TILE), rows)

        def column(which):
            return pl.ds(pl.multiple_of(which * inner + p * lanes, lanes), lanes)

        def cum(h):
            return cumx[m, :, pl.ds(pl.multiple_of((2 * p + h) * lanes, lanes), lanes)]

        return m, p, span, column, cum

    @pl.loop(0, micro * pairs)
    def _(u):
        m, p, span, column, cum = located(u)
        both = jnp.where(first_half, cum(0), cum(1))
        ending = both[rows - 1 :, :]
        scaled = (proj[span, column(1)].astype(f32) * jnp.exp(ending - both)).astype(bf16)
        state = dot(scaled, proj[span, column(2)], ((0,), (0,)))
        packed = jnp.where(first_item, state[:head_dim], state[head_dim:]).astype(bf16)
        weight = jnp.broadcast_to(jnp.exp(ending), (TILE, lanes)).astype(bf16)
        for piece in range(per_pair):
            items[u * per_pair + piece, :part, :] = packed[piece * part : (piece + 1) * part]
            items[u * per_pair + piece, part:, :] = weight

    def first(to, slot_from):
        return pltpu.make_async_remote_copy(
            src_ref=items.at[to],
            dst_ref=got.at[slot_from],
            send_sem=s1.at[to],
            recv_sem=r1.at[slot_from],
            device_id={"ctx": to},
            device_id_type=MESH,
        )

    def second(to, slot_from):
        return pltpu.make_async_remote_copy(
            src_ref=carried.at[to],
            dst_ref=landed.at[slot_from],
            send_sem=s2.at[to],
            recv_sem=r2.at[slot_from],
            device_id={"ctx": to},
            device_id_type=MESH,
        )

    @pl.loop(1, total)
    def _(k):
        first(lax.rem(me + k, total), me).start()

    got[me] = items[me]

    @pl.loop(0, micro * pairs)
    def _(u):
        m, p, span, column, cum = located(u)
        queries, keys, values = (proj[span, column(i)] for i in range(3))
        outs = []
        for h in range(2):
            own_half = first_half if h == 0 else jnp.logical_not(first_half)
            scores = dot(jnp.where(own_half, queries, jnp.zeros_like(queries)), keys, ((1,), (1,)))
            gap = cum(h) - cumt[m, pl.ds(2 * p + h, 1), :]
            weights = jnp.where(
                causal, scores * jnp.exp(jnp.where(causal, gap, 0.0)), 0.0
            ).astype(bf16)
            outs.append(dot(weights, values))
        intra[span, column(0)] = jnp.where(first_half, outs[0], outs[1])

    def step(b, acc):
        @pl.when(b != me)
        def _():
            first(b, b).wait_recv()

        low = acc.astype(bf16)
        carried[b] = low

        @pl.when(b != me)
        def _():
            second(b, me).start()

        @pl.when(b == me)
        def _():
            landed[me] = low

        item = got[b].astype(f32)
        return acc * item[part : part + 1] + item[:part]

    lax.fori_loop(0, total, step, jnp.zeros((part, lanes), f32))

    @pl.loop(1, total)
    def _(k):
        peer = lax.rem(me + k, total)
        second(peer, peer).wait_recv()

    @pl.loop(0, micro * pairs)
    def _(u):
        m, p, span, column, cum = located(u)
        low = jnp.concatenate([landed[u * per_pair + i] for i in range(per_pair)], axis=0)
        none = jnp.zeros_like(low)
        block = jnp.concatenate(
            [jnp.where(first_item, low, none), jnp.where(first_item, none, low)], axis=0
        )
        both = jnp.where(first_half, cum(0), cum(1))
        mixture = intra[span, column(0)] + dot(proj[span, column(0)], block) * jnp.exp(both)
        squares = mixture * mixture
        scales = [
            lax.rsqrt(
                jnp.sum(jnp.where(own, squares, 0.0), axis=-1, keepdims=True) / head_dim + 1e-05
            )
            for own in (first_half, jnp.logical_not(first_half))
        ]
        mixed[span, column(0)] = (mixture * jnp.where(first_half, scales[0], scales[1])).astype(bf16)

    @pl.loop(0, width // 256)
    def _(c):
        cols = pl.ds(pl.multiple_of(c * 256, 256), 256)
        product = dot(mixed[...], full_b[:, cols])
        for m in range(micro):
            result[m, :, cols] = (
                xbuf[m, :, cols].astype(f32) + product[m * rows : (m + 1) * rows]
            ).astype(bf16)

    @pl.when(section < sections - 1)
    def _():
        pass_on.start()

    put = pltpu.make_async_copy(result, out, own_sem.at[3])
    put.start()

    for index in range(len(parts)):
        onward(me, mine, index, True, lambda c: c.wait_send())

    @pl.loop(1, total)
    def _(j):
        source, coords = source_of(j)
        for index in range(len(parts)):
            onward(source, coords, index, False, lambda c: c.wait_send())

    @pl.loop(1, total)
    def _(k):
        peer = lax.rem(me + k, total)
        first(peer, me).wait_send()
        second(peer, me).wait_send()

    put.wait()

    @pl.when(section < sections - 1)
    def _():
        pass_on.wait_send()


GATE = 1


def shards(sizes, sections, tokens, qkv_weight, out_weight, log_decay):
    micro, rows, width = tokens.shape
    total = int(np.prod(sizes))
    heads = log_decay.shape[3]
    own = (qkv_weight[0], out_weight[0])
    inner = own[1].shape[0] * total
    lanes = 2 * inner // heads
    part = micro * inner // 2 // total
    plan = [pieces(s.shape[0], sizes) for s in own]
    count = sum(len(p) for p in plan)
    slots = sum(1 if s == 2 else 2 for s in sizes)
    f32, bf16 = jnp.float32, jnp.bfloat16
    dma = pltpu.SemaphoreType.DMA
    anywhere = pl.BlockSpec(memory_space=pl.ANY)
    vmem = pl.BlockSpec(memory_space=pltpu.VMEM)
    result = pl.pallas_call(
        functools.partial(whole_kernel, sizes, sections, plan, heads),
        out_shape=jax.ShapeDtypeStruct(tokens.shape, tokens.dtype),
        in_specs=[anywhere, vmem, anywhere, anywhere],
        out_specs=anywhere,
        scratch_shapes=[
            pltpu.VMEM((own[0].shape[0] * total, own[0].shape[1]), bf16),
            pltpu.VMEM((own[1].shape[0] * total, own[1].shape[1]), bf16),
            pltpu.VMEM((micro, rows, width), bf16),
            pltpu.VMEM((micro * rows, width), bf16),
            pltpu.VMEM((micro * rows, 3 * inner), bf16),
            pltpu.VMEM((micro, rows, heads * lanes), f32),
            pltpu.VMEM((micro, heads, rows), f32),
            pltpu.VMEM((micro * rows, inner), f32),
            pltpu.VMEM((micro * rows, inner), bf16),
            pltpu.VMEM((micro, rows, width), bf16),
            pltpu.VMEM((total, part + TILE, lanes), bf16),
            pltpu.VMEM((total, part + TILE, lanes), bf16),
            pltpu.VMEM((total, part, lanes), bf16),
            pltpu.VMEM((total, part, lanes), bf16),
            dma((total, count, slots)),
            dma((total, count)),
            dma((4,)),
            dma((1,)),
            dma((1,)),
            pltpu.SemaphoreType.REGULAR,
            dma((total,)),
            dma((total,)),
            dma((total,)),
            dma((total,)),
        ],
        compiler_params=pltpu.CompilerParams(
            collective_id=0, has_side_effects=True, vmem_limit_bytes=60 * 2**20
        ),
        name="mixer_stack",
    )(tokens, log_decay[0], *own)
    return result[None]


def solution(mesh):
    in_specs = (
        P(None, "ctx", None),
        P("section", "ctx", None),
        P("section", "ctx", None),
        P("section", None, "ctx", None),
    )
    out_specs = P("section", None, "ctx", None)
    return jax.shard_map(
        functools.partial(shards, line_sizes(mesh), mesh.shape["section"]),
        mesh=mesh,
        in_specs=in_specs,
        out_specs=out_specs,
        check_vma=False,
    )
```

```python
import functools

import jax
import jax.numpy as jnp
import numpy as np
from jax import lax
from jax.experimental import pallas as pl
from jax.experimental.pallas import tpu as pltpu
from jax.sharding import PartitionSpec as P

MESH = pl.DeviceIdType.MESH
TILE = 16


def line_sizes(mesh):
    total = mesh.shape["ctx"]
    places = np.moveaxis(mesh.devices, mesh.axis_names.index("ctx"), 0).reshape(total, -1)[:, 0]
    sizes, left = [], total
    try:
        coords = [tuple(d.coords) for d in places]
    except AttributeError:
        coords = None
    if coords is not None:
        step = 1
        while step < total:
            changed = [a != b for a, b in zip(coords[0], coords[step])]
            axis = changed.index(True)
            size = 1
            while step * size < total and (
                size == 1 or (coords[step * size][axis] != coords[0][axis]
                and all(coords[step * size][i] == coords[0][i] for i in range(3) if i != axis))
            ):
                size += 1
            while total % (step * size):
                size -= 1
            sizes.insert(0, size)
            step *= size
    else:
        while left > 1:
            sizes.append(2)
            left //= 2
    return tuple(sizes)


def routes(sizes):
    d = len(sizes)
    if d != 3:
        return [(tuple(range(d)), 1)]
    return [((0, 2, 1), 3), ((0, 1, 2), 3), ((2, 1, 0), 1), ((1, 2, 0), 1)]


def pieces(rows, sizes):
    orders = routes(sizes)
    units = rows // TILE
    if len(orders) == 1 or units < 2:
        return [(orders[0][0], 0, rows)]
    shares = [units // 2, units - units // 2] if units < 8 else None
    if shares is None:
        whole = sum(s for _, s in orders)
        shares = [s * units // whole for _, s in orders]
        shares[0] += units - sum(shares)
    out, at = [], 0
    for (order, _), share in zip(orders, shares):
        out.append((order, at * TILE, share * TILE))
        at += share
    return out


def place_in_line(me, size, t):
    low = jnp.minimum(me, size - 1 - me)
    half = lax.div(t + 1, 2)
    near = jnp.where(lax.rem(t, 2) == 1, me + half, me - half)
    far = jnp.where(me < size - 1 - me, me + (t - low), me - (t - low))
    return jnp.where(t <= 2 * low, near, far)


def dot(a, b, contract=((1,), (0,)), precision=None):
    return lax.dot_general(
        a, b, (contract, ((), ())), precision=precision, preferred_element_type=jnp.float32
    )


def whole_kernel(
    sizes, sections, plan, heads, tokens, decay, shard_a, shard_b, out,
    full_a, full_b, xbuf, normed, proj, cumx, cumt, intra, mixed, result, items, got, carried,
    landed, send_sem, recv_sem, own_sem, x_send, x_recv, start_sem, s1, r1, s2, r2,
):
    f32, bf16 = jnp.float32, jnp.bfloat16
    shards, wholes = (shard_a, shard_b), (full_a, full_b)
    count = 2
    d = len(sizes)
    total = int(np.prod(sizes))
    strides = [int(np.prod(sizes[i + 1 :])) for i in range(d)]
    me = lax.axis_index("ctx")
    section = lax.axis_index("section")
    mine = [lax.rem(lax.div(me, strides[i]), sizes[i]) for i in range(d)]
    slots, ways = 0, []
    for i in range(d):
        for sign in (1, -1):
            ways.append((i, sign, slots if sizes[i] == 2 or sign == 1 else slots + 1))
        slots += 1 if sizes[i] == 2 else 2
    micro, rows, width = xbuf.shape
    inner = mixed.shape[1]
    head_dim = inner // heads
    pairs = heads // 2
    lanes = 2 * head_dim
    part = items.shape[1] - TILE

    barrier = pltpu.get_barrier_semaphore()

    @pl.loop(1, total)
    def _(k):
        pl.semaphore_signal(
            barrier, inc=1, device_id={"ctx": lax.rem(me + k, total)}, device_id_type=MESH
        )

    @pl.when(section > 0)
    def _():
        pl.semaphore_signal(barrier, inc=1, device_id={"section": section - 1}, device_id_type=MESH)

    @pl.when(section < sections - 1)
    def _():
        pl.semaphore_signal(barrier, inc=1, device_id={"section": section + 1}, device_id_type=MESH)

    greeted = (section > 0).astype(jnp.int32) + (section < sections - 1).astype(jnp.int32)
    pl.semaphore_wait(barrier, greeted + (total - 1))

    parts = [(a, order, at, size) for a in range(count) for order, at, size in plan[a]]

    def copy(source, index, way, own):
        a, _, at, size = parts[index]
        i, sign, slot = way
        depth = shards[a].shape[0]
        begin = pl.multiple_of(source * depth + at, TILE)
        target = wholes[a].at[pl.ds(begin, size)]
        return pltpu.make_async_remote_copy(
            src_ref=shards[a].at[pl.ds(at, size)] if own else target,
            dst_ref=target,
            send_sem=send_sem.at[source, index, slot],
            recv_sem=recv_sem.at[source, index],
            device_id={"ctx": me + sign * strides[i]},
            device_id_type=MESH,
        )

    def onward(source, coords, index, own, act):
        order = parts[index][1]
        for way in ways:
            i, sign, _ = way
            ok = jnp.logical_and(mine[i] + sign >= 0, mine[i] + sign < sizes[i])
            if not own:
                here = coords[i]
                ok = jnp.logical_and(ok, (mine[i] - here) * sign >= 0)
                for later in order[order.index(i) + 1 :]:
                    ok = jnp.logical_and(ok, mine[later] == coords[later])

            @pl.when(ok)
            def _(way=way):
                act(copy(source, index, way, own))

    own_copies = []
    for a in range(count):
        depth = shards[a].shape[0]
        own_copies.append(
            pltpu.make_async_copy(
                shards[a],
                wholes[a].at[pl.ds(pl.multiple_of(me * depth, TILE), depth)],
                own_sem.at[a],
            )
        )
        own_copies[-1].start()

    x_own = pltpu.make_async_copy(tokens, xbuf, own_sem.at[2])

    @pl.when(section == 0)
    def _():
        x_own.start()

    @pl.when(section > 0)
    def _():
        pl.semaphore_wait(start_sem, 1)

    for index in range(len(parts)):
        onward(me, mine, index, True, lambda c: c.start())

    at_row = lax.broadcasted_iota(jnp.int32, (rows, rows), 0)
    at_col = lax.broadcasted_iota(jnp.int32, (rows, rows), 1)
    causal = at_row >= at_col
    lower = causal.astype(f32)
    for m in range(micro):
        spread = (
            lax.broadcasted_iota(jnp.int32, (heads, heads * lanes), 0)
            == lax.broadcasted_iota(jnp.int32, (heads, heads * lanes), 1) // lanes
        ).astype(f32)
        own = decay[m]
        summed = dot(lower, own, precision=lax.Precision.HIGHEST)
        cumx[m] = dot(summed, spread, precision=lax.Precision.HIGHEST)
        cumt[m] = dot(own.T, lower, ((1,), (1,)), precision=lax.Precision.HIGHEST)

    def source_of(j):
        coords = [
            place_in_line(mine[i], sizes[i], lax.rem(lax.div(j, strides[i]), sizes[i]))
            for i in range(d)
        ]
        source = sum(c * s for c, s in zip(coords, strides))
        return source, coords

    def receive(wanted, least, most):
        @pl.loop(least * total, most * total)
        def _(k):
            hops, j = lax.div(k, total), lax.rem(k, total)
            source, coords = source_of(j)
            away = sum(jnp.abs(mine[i] - coords[i]) for i in range(d))

            @pl.when(away == hops)
            def _():
                for index in range(len(parts)):
                    if parts[index][0] == wanted:
                        copy(source, index, ways[0], False).wait_recv()
                        onward(source, coords, index, False, lambda c: c.start())

    farthest = sum(n - 1 for n in sizes) + 1

    def let_next_start():
        @pl.when(section < sections - 1)
        def _():
            pl.semaphore_signal(
                start_sem, inc=1, device_id={"section": section + 1}, device_id_type=MESH
            )

    def normalize():
        @pl.loop(0, micro * (rows // TILE))
        def _(r):
            m, q = lax.div(r, rows // TILE), lax.rem(r, rows // TILE)
            wide = xbuf[m, pl.ds(pl.multiple_of(q * TILE, TILE), TILE), :].astype(f32)
            scale = lax.rsqrt(jnp.mean(wide * wide, axis=-1, keepdims=True) + 1e-05)
            normed[pl.ds(pl.multiple_of(r * TILE, TILE), TILE), :] = (wide * scale).astype(bf16)

    @pl.when(section == 0)
    def _():
        x_own.wait()
        normalize()

    receive(0, 1, farthest)

    let_next_start()
    for c in own_copies:
        c.wait()

    pass_on = pltpu.make_async_remote_copy(
        src_ref=result,
        dst_ref=xbuf,
        send_sem=x_send.at[0],
        recv_sem=x_recv.at[0],
        device_id={"section": lax.rem(section + 1, sections)},
        device_id_type=MESH,
    )

    @pl.when(section > 0)
    def _():
        receive(1, 1, farthest)
        pass_on.wait_recv()
        normalize()

    @pl.loop(0, 3 * inner // 256)
    def _(c):
        cols = pl.ds(pl.multiple_of(c * 256, 256), 256)
        proj[:, cols] = dot(normed[...], full_a[:, cols]).astype(bf16)

    first_half = lax.broadcasted_iota(jnp.int32, (rows, lanes), 1) < head_dim
    first_item = lax.broadcasted_iota(jnp.int32, (head_dim, lanes), 1) < head_dim
    per_pair = head_dim // part

    def located(u):
        m, p = lax.div(u, pairs), lax.rem(u, pairs)
        span = pl.ds(pl.multiple_of(m * rows, TILE), rows)

        def column(which):
            return pl.ds(pl.multiple_of(which * inner + p * lanes, lanes), lanes)

        def cum(h):
            return cumx[m, :, pl.ds(pl.multiple_of((2 * p + h) * lanes, lanes), lanes)]

        return m, p, span, column, cum

    @pl.loop(0, micro * pairs)
    def _(u):
        m, p, span, column, cum = located(u)
        both = jnp.where(first_half, cum(0), cum(1))
        ending = both[rows - 1 :, :]
        scaled = (proj[span, column(1)].astype(f32) * jnp.exp(ending - both)).astype(bf16)
        state = dot(scaled, proj[span, column(2)], ((0,), (0,)))
        packed = jnp.where(first_item, state[:head_dim], state[head_dim:]).astype(bf16)
        weight = jnp.broadcast_to(jnp.exp(ending), (TILE, lanes)).astype(bf16)
        for piece in range(per_pair):
            items[u * per_pair + piece, :part, :] = packed[piece * part : (piece + 1) * part]
            items[u * per_pair + piece, part:, :] = weight

    def first(to, slot_from):
        return pltpu.make_async_remote_copy(
            src_ref=items.at[to],
            dst_ref=got.at[slot_from],
            send_sem=s1.at[to],
            recv_sem=r1.at[slot_from],
            device_id={"ctx": to},
            device_id_type=MESH,
        )

    def second(to, slot_from):
        return pltpu.make_async_remote_copy(
            src_ref=carried.at[to],
            dst_ref=landed.at[slot_from],
            send_sem=s2.at[to],
            recv_sem=r2.at[slot_from],
            device_id={"ctx": to},
            device_id_type=MESH,
        )

    @pl.loop(1, total)
    def _(k):
        first(lax.rem(me + k, total), me).start()

    got[me] = items[me]

    def within(u):
        m, p, span, column, cum = located(u)
        queries, keys, values = (proj[span, column(i)] for i in range(3))
        outs = []
        for h in range(2):
            own_half = first_half if h == 0 else jnp.logical_not(first_half)
            scores = dot(jnp.where(own_half, queries, jnp.zeros_like(queries)), keys, ((1,), (1,)))
            gap = cum(h) - cumt[m, pl.ds(2 * p + h, 1), :]
            weights = jnp.where(
                causal, scores * jnp.exp(jnp.where(causal, gap, 0.0)), 0.0
            ).astype(bf16)
            outs.append(dot(weights, values))
        intra[span, column(0)] = jnp.where(first_half, outs[0], outs[1])

    @pl.when(section == 0)
    def _():
        receive(1, 1, 2)

    @pl.loop(0, micro * pairs)
    def _(u):
        within(u)

    @pl.when(section == 0)
    def _():
        receive(1, 2, 3)

    def step(b, acc):
        @pl.when(b != me)
        def _():
            first(b, b).wait_recv()

        low = acc.astype(bf16)
        carried[b] = low

        @pl.when(b != me)
        def _():
            second(b, me).start()

        @pl.when(b == me)
        def _():
            landed[me] = low

        item = got[b].astype(f32)
        return acc * item[part : part + 1] + item[:part]

    lax.fori_loop(0, total, step, jnp.zeros((part, lanes), f32))

    @pl.when(section == 0)
    def _():
        receive(1, 3, farthest)

    @pl.loop(1, total)
    def _(k):
        peer = lax.rem(me + k, total)
        second(peer, peer).wait_recv()

    @pl.loop(0, micro * pairs)
    def _(u):
        m, p, span, column, cum = located(u)
        low = jnp.concatenate([landed[u * per_pair + i] for i in range(per_pair)], axis=0)
        none = jnp.zeros_like(low)
        block = jnp.concatenate(
            [jnp.where(first_item, low, none), jnp.where(first_item, none, low)], axis=0
        )
        both = jnp.where(first_half, cum(0), cum(1))
        mixture = intra[span, column(0)] + dot(proj[span, column(0)], block) * jnp.exp(both)
        squares = mixture * mixture
        scales = [
            lax.rsqrt(
                jnp.sum(jnp.where(own, squares, 0.0), axis=-1, keepdims=True) / head_dim + 1e-05
            )
            for own in (first_half, jnp.logical_not(first_half))
        ]
        mixed[span, column(0)] = (mixture * jnp.where(first_half, scales[0], scales[1])).astype(bf16)

    @pl.loop(0, width // 256)
    def _(c):
        cols = pl.ds(pl.multiple_of(c * 256, 256), 256)
        product = dot(mixed[...], full_b[:, cols])
        for m in range(micro):
            result[m, :, cols] = (
                xbuf[m, :, cols].astype(f32) + product[m * rows : (m + 1) * rows]
            ).astype(bf16)

    @pl.when(section < sections - 1)
    def _():
        pass_on.start()

    put = pltpu.make_async_copy(result, out, own_sem.at[3])
    put.start()

    for index in range(len(parts)):
        onward(me, mine, index, True, lambda c: c.wait_send())

    @pl.loop(1, total)
    def _(j):
        source, coords = source_of(j)
        for index in range(len(parts)):
            onward(source, coords, index, False, lambda c: c.wait_send())

    @pl.loop(1, total)
    def _(k):
        peer = lax.rem(me + k, total)
        first(peer, me).wait_send()
        second(peer, me).wait_send()

    put.wait()

    @pl.when(section < sections - 1)
    def _():
        pass_on.wait_send()


def shards(sizes, sections, tokens, qkv_weight, out_weight, log_decay):
    micro, rows, width = tokens.shape
    total = int(np.prod(sizes))
    heads = log_decay.shape[3]
    own = (qkv_weight[0], out_weight[0])
    inner = own[1].shape[0] * total
    lanes = 2 * inner // heads
    part = micro * inner // 2 // total
    plan = [pieces(s.shape[0], sizes) for s in own]
    count = sum(len(p) for p in plan)
    slots = sum(1 if s == 2 else 2 for s in sizes)
    f32, bf16 = jnp.float32, jnp.bfloat16
    dma = pltpu.SemaphoreType.DMA
    anywhere = pl.BlockSpec(memory_space=pl.ANY)
    vmem = pl.BlockSpec(memory_space=pltpu.VMEM)
    result = pl.pallas_call(
        functools.partial(whole_kernel, sizes, sections, plan, heads),
        out_shape=jax.ShapeDtypeStruct(tokens.shape, tokens.dtype),
        in_specs=[anywhere, vmem, anywhere, anywhere],
        out_specs=anywhere,
        scratch_shapes=[
            pltpu.VMEM((own[0].shape[0] * total, own[0].shape[1]), bf16),
            pltpu.VMEM((own[1].shape[0] * total, own[1].shape[1]), bf16),
            pltpu.VMEM((micro, rows, width), bf16),
            pltpu.VMEM((micro * rows, width), bf16),
            pltpu.VMEM((micro * rows, 3 * inner), bf16),
            pltpu.VMEM((micro, rows, heads * lanes), f32),
            pltpu.VMEM((micro, heads, rows), f32),
            pltpu.VMEM((micro * rows, inner), f32),
            pltpu.VMEM((micro * rows, inner), bf16),
            pltpu.VMEM((micro, rows, width), bf16),
            pltpu.VMEM((total, part + TILE, lanes), bf16),
            pltpu.VMEM((total, part + TILE, lanes), bf16),
            pltpu.VMEM((total, part, lanes), bf16),
            pltpu.VMEM((total, part, lanes), bf16),
            dma((total, count, slots)),
            dma((total, count)),
            dma((4,)),
            dma((1,)),
            dma((1,)),
            pltpu.SemaphoreType.REGULAR,
            dma((total,)),
            dma((total,)),
            dma((total,)),
            dma((total,)),
        ],
        compiler_params=pltpu.CompilerParams(
            collective_id=0, has_side_effects=True, vmem_limit_bytes=60 * 2**20
        ),
        name="mixer_stack",
    )(tokens, log_decay[0], *own)
    return result[None]


def solution(mesh):
    in_specs = (
        P(None, "ctx", None),
        P("section", "ctx", None),
        P("section", "ctx", None),
        P("section", None, "ctx", None),
    )
    out_specs = P("section", None, "ctx", None)
    return jax.shard_map(
        functools.partial(shards, line_sizes(mesh), mesh.shape["section"]),
        mesh=mesh,
        in_specs=in_specs,
        out_specs=out_specs,
        check_vma=False,
    )
```
